32 devices in a mesh: groups: 2 (over y), seq: 4 (over z), inner: 2 (over x), batch: 2 (over core).
Axes of the slice: x: 2, y: 2, z: 4, core: 2. Of those that a mesh axis runs over, the one named last changes fastest.
Arguments:
- queries: bfloat16 [4, 2048, 256], P(('groups', 'batch'), ('seq', 'inner')), parts along dimension 0, may hold values from -6 to 6
- keys: bfloat16 [4, 2048, 256], P(('groups', 'batch'), ('seq', 'inner')), parts along dimension 0, may hold values from -6 to 6
- values: bfloat16 [4, 2048, 256], P(('groups', 'batch'), ('seq', 'inner')), parts along dimension 0, may hold values from -6 to 6
- rates: float32 [4, 2048], P(('groups', 'batch'), ('seq', 'inner')), parts along dimension 0, may hold values from 0.05 to 1
- video_start: int32 [4], P(('groups', 'batch')), parts along dimension 0, may hold values from 0 to 511
- span_len: int32 [4, 4], P(('groups', 'batch'), 'seq'), parts along dimension 0, may hold values from 256 to 512, as said below
- init_weights: float32 [3, 256, 256], replicated, may hold values from -0.375 to 0.375
Outputs:
- outputs: bfloat16 [4, 2048, 256], P(('groups', 'batch'), ('seq', 'inner')), parts along dimension 0
- final_weights: float32 [4, 3, 256, 256], P(('groups', 'batch'), None, 'seq'), parts along dimension 0
The draws below stay inside these ranges and needn't reach their ends.
There are 2 independent parts, one for each index of `groups`. The reference program is written for one: setup_inputs(seed, part) draws one part's arguments, and reference() takes and returns one part's arrays. A program takes and returns all parts, laid end to end along the dimension named above; an argument that names none is the same for every part. Nothing has to cross between parts.
Inputs may be any that keep to these rules, and one draw needn't show every extreme that they name: Every video has at least one span with span_len equal to 512.
All inputs are finite; a program needn't handle non-finite values.
Results may differ from the reference program's by a relative error of at most 0.015.
Values may be sent and summed in bfloat16 or wider, within the bound.
A program may use at most 64 MiB of HBM per device.

```python
import math
import jax
import jax.numpy as jnp
from jax import lax

HEAD = 256
HIDDEN_SIZE = 256
TOK_DEV = 256
NS_STEPS = 5
SPAN = 512
LENGTH = 2048
VIDEOS = 2
N_SEQ = 4
N_INNER = 2


def draw_span_len(key, part):
    drawn_len = jax.random.randint(jax.random.fold_in(key, 11), (VIDEOS, N_SEQ), SPAN // 2, SPAN + 1)
    chosen = jax.random.randint(jax.random.fold_in(key, 12), (VIDEOS, 1), 0, N_SEQ)
    full_mask = jnp.arange(N_SEQ, dtype=jnp.int32)[None, :] == chosen
    return jnp.where(full_mask, SPAN, drawn_len).astype(jnp.int32)


def levels(rng, dims, cuts, low, top_value):
    level, own = 1.0, jax.random.fold_in(rng, 6)
    for dim, blocks in cuts:
        steps = jnp.exp(jax.random.uniform(jax.random.fold_in(own, dim), (blocks,), jnp.float32, low / len(cuts), top_value / len(cuts)))
        level = level * jnp.repeat(steps, dims[dim] // blocks).reshape([-1 if axis == dim else 1 for axis in range(len(dims))])
    return level


def centred(rng, extent, scale, bound, cuts=(), kind=jnp.bfloat16):
    loudness = levels(rng, extent, cuts, -0.22, 0.18) if cuts else 1.0
    values = jax.random.normal(rng, extent, jnp.float32) * scale * loudness
    return jnp.minimum(jnp.maximum(values, -bound), bound).astype(kind)


def setup_inputs(seed: int = 0, part: int = 0) -> dict:
    arg_keys = jax.random.split(jax.random.key(seed), 8)
    own_keys = jax.random.split(jax.random.fold_in(arg_keys[7], part), 8)
    return {
        "queries": centred(own_keys[0], (VIDEOS, LENGTH, HEAD), 1.0, 6.0, ((0, 2), (1, 8))),
        "keys": centred(own_keys[1], (VIDEOS, LENGTH, HEAD), 1.0, 6.0, ((0, 2), (1, 8))),
        "values": centred(own_keys[2], (VIDEOS, LENGTH, HEAD), 1.0, 6.0, ((0, 2), (1, 8))),
        "rates": jnp.clip(jnp.exp(math.log(1.0) - 2.9957323 * jax.random.uniform(own_keys[3], (VIDEOS, LENGTH), jnp.float32) ** levels(own_keys[3], (VIDEOS, LENGTH), ((0, 2), (1, 8)), -0.2, 0.2)), 0.05, 1.0),
        "video_start": jax.random.randint(own_keys[4], (VIDEOS,), 0, SPAN).astype(jnp.int32),
        "span_len": draw_span_len(jax.random.fold_in(jax.random.fold_in(arg_keys[7], part), 71), part),
        "init_weights": centred(arg_keys[6], (3, HEAD, HIDDEN_SIZE), HEAD ** -0.5, 0.375, (), jnp.float32),
    }


step_size = 0.1
norm_eps = 1e-07
column_eps = 1e-06

def swish_parts(pre_act):
    sigma = jax.nn.sigmoid(pre_act)
    return (pre_act * sigma, sigma * (1.0 + pre_act * (1.0 - sigma)))

def apply_net(rows, half_weights):
    gate_pre = jnp.dot(rows, half_weights[0], preferred_element_type=jnp.float32)
    up_pre = jnp.dot(rows, half_weights[1], preferred_element_type=jnp.float32)
    active_part, unused_slope = swish_parts(gate_pre)
    hidden = (active_part * up_pre).astype(jnp.bfloat16)
    contract = (((1,), (1,)), ((), ()))
    return lax.dot_general(hidden, half_weights[2], contract, preferred_element_type=jnp.float32).astype(jnp.bfloat16)

def key_grads(key_rows, value_rows, weight, half_weights):
    gate_pre = jnp.dot(key_rows, half_weights[0], preferred_element_type=jnp.float32)
    up_pre = jnp.dot(key_rows, half_weights[1], preferred_element_type=jnp.float32)
    active_part, slope_term = swish_parts(gate_pre)
    hidden = (active_part * up_pre).astype(jnp.bfloat16)
    neg_values = (-(weight[:, None] * value_rows.astype(jnp.float32))).astype(jnp.bfloat16)
    back_grad = jnp.dot(neg_values, half_weights[2], preferred_element_type=jnp.float32)
    d_upper = (back_grad * active_part).astype(jnp.bfloat16)
    d_gate = (back_grad * up_pre * slope_term).astype(jnp.bfloat16)
    contract = (((0,), (0,)), ((), ()))
    grad_one = lax.dot_general(key_rows, d_gate, contract, preferred_element_type=jnp.float32)
    grad_three = lax.dot_general(key_rows, d_upper, contract, preferred_element_type=jnp.float32)
    grad_two = lax.dot_general(neg_values, hidden, contract, preferred_element_type=jnp.float32)
    return jnp.stack([grad_one, grad_three, grad_two])

def newton(grad):
    scale = jnp.sqrt(jnp.sum(grad * grad))
    iterate = grad / (scale + norm_eps)
    for unused in range(NS_STEPS):
        gram = jnp.dot(iterate, iterate.T, precision=lax.Precision.HIGHEST, preferred_element_type=jnp.float32)
        iterate = 1.5 * iterate - 0.5 * jnp.dot(gram, iterate, precision=lax.Precision.HIGHEST, preferred_element_type=jnp.float32)
    return iterate.astype(jnp.bfloat16)

def renorm(before, moved):
    old_norm = jnp.sqrt(lax.optimization_barrier(jnp.sum(before * before, axis=1, keepdims=True)) + column_eps)
    new_norm = jnp.sqrt(lax.optimization_barrier(jnp.sum(moved * moved, axis=1, keepdims=True)) + column_eps)
    return moved * (old_norm / new_norm)

def reference(queries, keys, values, rates, video_start, span_len, init_weights):

    def one_video(pieces):
        query_all, key_all, value_all, rate_all, begin, lengths = pieces

        def span_step(state, span_pieces):
            query_rows, key_rows, value_rows, rate_rows, length, span_index = span_pieces
            half_weights = state.astype(jnp.bfloat16)
            out_rows = apply_net(query_rows, half_weights)
            within = jnp.arange(SPAN, dtype=jnp.int32)
            position = span_index * SPAN + within
            valid = ((position >= begin) & (within < length)).astype(jnp.float32)
            weight = rate_rows * valid
            total = jnp.zeros(state.shape, jnp.float32)
            for shard in range(N_INNER):
                lower = shard * TOK_DEV
                partial_value = key_grads(key_rows[lower:lower + TOK_DEV], value_rows[lower:lower + TOK_DEV], weight[lower:lower + TOK_DEV], half_weights)
                rounded = lax.optimization_barrier(partial_value.astype(jnp.bfloat16))
                total = total + rounded.astype(jnp.float32)
            ortho = jnp.stack([newton(total[which]) for which in range(3)])
            new_state = renorm(state, state - step_size * ortho.astype(jnp.float32))
            return (new_state, out_rows)
        final_state, outs = lax.scan(span_step, init_weights, (query_all.reshape(N_SEQ, SPAN, HEAD), key_all.reshape(N_SEQ, SPAN, HEAD), value_all.reshape(N_SEQ, SPAN, HEAD), rate_all.reshape(N_SEQ, SPAN), lengths, jnp.arange(N_SEQ, dtype=jnp.int32)))
        return (outs.reshape(LENGTH, HEAD), final_state)
    outputs, final_weights = lax.map(one_video, (queries, keys, values, rates, video_start, span_len))
    return (outputs, final_weights)
```

```python
import functools

import jax
import jax.numpy as jnp
from jax import lax
from jax.experimental import pallas as pl
from jax.experimental.pallas import tpu as pltpu
from jax.sharding import PartitionSpec as P

NS_STEPS = 5
step_size = 0.1
norm_eps = 1e-07
column_eps = 1e-06
F32, BF16 = jnp.float32, jnp.bfloat16


def dot(a, b, ca, cb):
    return lax.dot_general(a, b, (((ca,), (cb,)), ((), ())), preferred_element_type=F32)


def apply_net(rows, w1, w3, w2):
    gate = dot(rows, w1, 1, 0)
    up = dot(rows, w3, 1, 0)
    hidden = (gate * jax.nn.sigmoid(gate) * up).astype(BF16)
    return dot(hidden, w2, 1, 1).astype(BF16)


def span_grads(k, nv, w1, w3, w2):
    gate = dot(k, w1, 1, 0)
    up = dot(k, w3, 1, 0)
    back = dot(nv, w2, 1, 0)
    s = jax.nn.sigmoid(gate)
    active = gate * s
    hidden = (active * up).astype(BF16)
    d_up = (back * active).astype(BF16)
    d_gate = (back * up * (s * (1.0 + gate * (1.0 - s)))).astype(BF16)
    return [dot(k, d_gate, 0, 0), dot(k, d_up, 0, 0), dot(nv, hidden, 0, 0)]


def newton(grads):
    xs = [g * (1.0 / (jnp.sqrt(jnp.sum(g * g, keepdims=True)) + norm_eps)) for g in grads]
    for unused in range(NS_STEPS):
        halves = [x.astype(BF16) for x in xs]
        grams = [dot(h, h, 1, 1).astype(BF16) for h in halves]
        xs = [1.5 * x - 0.5 * dot(g, h, 1, 0) for x, g, h in zip(xs, grams, halves)]
    return xs


def chain_step(c, me, kv_ref, q_ref, state_ref, norm_ref, out_ref):
    inner, pair, tok, head = kv_ref.shape[1:]
    w1, w3, w2 = [state_ref[i].astype(BF16) for i in range(3)]

    @pl.when(c == me)
    def _():
        out_ref[...] = apply_net(q_ref[...], w1, w3, w2)

    k = kv_ref[c, :, 0].reshape(inner * tok, head)
    nv = kv_ref[c, :, 1].reshape(inner * tok, head)
    xs = newton(span_grads(k, nv, w1, w3, w2))
    for i in range(3):
        moved = state_ref[i] - step_size * xs[i].astype(BF16).astype(F32)
        before = norm_ref[i]
        after = jnp.sum(moved * moved, axis=0, keepdims=True)
        ratio = (before + column_eps) / (after + column_eps)
        state_ref[i] = moved * jnp.sqrt(ratio)
        norm_ref[i] = after * ratio


def kernel(kv_ref, q_ref, init_ref, out_ref, final_ref, state_ref, norm_ref):
    seq_count = kv_ref.shape[0]
    me = lax.axis_index("seq")
    for i in range(3):
        w = init_ref[i]
        state_ref[i] = w
        norm_ref[i] = jnp.sum(w * w, axis=0, keepdims=True)

    @pl.loop(0, seq_count)
    def _(c):
        chain_step(c, me, kv_ref, q_ref, state_ref, norm_ref, out_ref)

    rows = final_ref.shape[1]
    final_ref[...] = state_ref[:, pl.ds(pl.multiple_of(me * rows, rows), rows), :]


def per_device(queries, keys, values, rates, video_start, span_len, init_weights):
    tok, head = queries.shape[1:]
    seq_count = lax.axis_size("seq")
    inner_count = lax.axis_size("inner")
    within = jnp.arange(tok, dtype=jnp.int32) + lax.axis_index("inner") * tok
    position = lax.axis_index("seq") * tok * inner_count + within
    valid = ((position >= video_start[0]) & (within < span_len[0, 0])).astype(F32)
    weight = rates[0] * valid
    nv = (-(weight[:, None] * values[0].astype(F32))).astype(BF16)
    kv = jnp.stack([keys[0], nv])
    kv = lax.all_gather(kv, ("seq", "inner"), axis=0, tiled=False)
    kv = kv.reshape(seq_count, inner_count, 2, tok, head)
    rows = init_weights.shape[1] // seq_count
    vm = pl.BlockSpec(memory_space=pltpu.VMEM)
    out, final = pl.pallas_call(
        kernel,
        out_shape=(
            jax.ShapeDtypeStruct((tok, head), BF16),
            jax.ShapeDtypeStruct((3, rows, init_weights.shape[2]), F32),
        ),
        in_specs=[vm] * 3,
        out_specs=(vm, vm),
        scratch_shapes=[
            pltpu.VMEM(init_weights.shape, F32),
            pltpu.VMEM((3, 1, init_weights.shape[2]), F32),
        ],
    )(kv, queries[0], init_weights)
    return out[None], final[None]


def solution(mesh):
    in_specs = (
        P(("groups", "batch"), ("seq", "inner"), None),
        P(("groups", "batch"), ("seq", "inner"), None),
        P(("groups", "batch"), ("seq", "inner"), None),
        P(("groups", "batch"), ("seq", "inner")),
        P(("groups", "batch")),
        P(("groups", "batch"), "seq"),
        P(),
    )
    out_specs = (
        P(("groups", "batch"), ("seq", "inner"), None),
        P(("groups", "batch"), None, "seq", None),
    )
    return jax.shard_map(
        per_device, mesh=mesh, in_specs=in_specs, out_specs=out_specs, check_vma=False
    )
```

```python
import functools

import jax
import jax.numpy as jnp
from jax import lax
from jax.experimental import pallas as pl
from jax.experimental.pallas import tpu as pltpu
from jax.sharding import PartitionSpec as P

NS_STEPS = 5
CHUNKS = 4
MESH = pl.DeviceIdType.MESH
step_size = 0.1
norm_eps = 1e-07
column_eps = 1e-06
F32, BF16 = jnp.float32, jnp.bfloat16


def dot(a, b, ca, cb):
    return lax.dot_general(a, b, (((ca,), (cb,)), ((), ())), preferred_element_type=F32)


def apply_net(rows, w1, w3, w2):
    gate = dot(rows, w1, 1, 0)
    up = dot(rows, w3, 1, 0)
    hidden = (gate * jax.nn.sigmoid(gate) * up).astype(BF16)
    return dot(hidden, w2, 1, 1).astype(BF16)


def span_grads(k, nv, w1, w3, w2):
    gate = dot(k, w1, 1, 0)
    up = dot(k, w3, 1, 0)
    back = dot(nv, w2, 1, 0)
    s = jax.nn.sigmoid(gate)
    active = gate * s
    hidden = (active * up).astype(BF16)
    d_up = (back * active).astype(BF16)
    d_gate = (back * up * (s * (1.0 + gate * (1.0 - s)))).astype(BF16)
    return [dot(k, d_gate, 0, 0), dot(k, d_up, 0, 0), dot(nv, hidden, 0, 0)]


def newton(grads):
    xs = [g * (1.0 / (jnp.sqrt(jnp.sum(g * g, keepdims=True)) + norm_eps)) for g in grads]
    for unused in range(NS_STEPS):
        halves = [x.astype(BF16) for x in xs]
        grams = [dot(h, h, 1, 1).astype(BF16) for h in halves]
        xs = [1.5 * x - 0.5 * dot(g, h, 1, 0) for x, g, h in zip(xs, grams, halves)]
    return xs


def kernel(
    n, m, start_ref, len_ref, key_ref, value_ref, rate_ref, q_ref, init_ref, out_ref, final_ref,
    kv, state, norm, grad, z_recv, up_send, down_send, x_recv, x_send,
):
    z, x = lax.axis_index("seq"), lax.axis_index("inner")
    tok = key_ref.shape[0]
    chunks, pair, part, head = kv.shape[2:]

    barrier = pltpu.get_barrier_semaphore()

    def greet(where):
        pl.semaphore_signal(barrier, inc=1, device_id=where, device_id_type=MESH)

    pl.when(z > 0)(lambda: greet({"seq": z - 1}))
    pl.when(z < n - 1)(lambda: greet({"seq": z + 1}))
    for r in range(1, m):
        greet({"inner": lax.rem(x + r, m)})

    within = lax.broadcasted_iota(jnp.int32, (1, tok), 1) + x * tok
    position = within + z * (tok * m)
    valid = ((position >= start_ref[0]) & (within < len_ref[0, 0])).astype(F32)
    weight = rate_ref[...] * valid
    eye = lax.broadcasted_iota(jnp.int32, (tok, tok), 0) == lax.broadcasted_iota(
        jnp.int32, (tok, tok), 1
    )
    column = jnp.sum(jnp.where(eye, weight, 0.0), axis=1, keepdims=True)
    neg = (-(column * value_ref[...].astype(F32))).astype(BF16)
    for j in range(chunks):
        kv[z, x, j, 0] = key_ref[j * part : (j + 1) * part, :]
        kv[z, x, j, 1] = neg[j * part : (j + 1) * part, :]
    for i in range(3):
        w = init_ref[i]
        state[i] = w
        norm[i] = jnp.sum(w * w, axis=0, keepdims=True)

    pl.semaphore_wait(barrier, (m - 1) + (z > 0).astype(jnp.int32) + (z < n - 1).astype(jnp.int32))

    def up(c, j):
        block = kv.at[c, x, j]
        return pltpu.make_async_remote_copy(
            block, block, up_send.at[c, j], z_recv.at[c, j], {"seq": z + 1}, MESH
        )

    def down(c, j):
        block = kv.at[c, x, j]
        return pltpu.make_async_remote_copy(
            block, block, down_send.at[c, j], z_recv.at[c, j], {"seq": z - 1}, MESH
        )

    def across(c, j, r):
        block = kv.at[c, x, j]
        return pltpu.make_async_remote_copy(
            block, block, x_send.at[r - 1, c, j], x_recv.at[r - 1, c, j],
            {"inner": lax.rem(x + r, m)}, MESH,
        )

    def send_across(c, j):
        for r in range(1, m):
            across(c, j, r).start()

    for j in range(chunks):
        early = (z < n - 1) & ((z == 0) | (j < 2 * z))
        pl.when(early)(lambda: up(z, j).start())
        pl.when(z > 0)(lambda: down(z, j).start())
        send_across(z, j)

    def phase(p):
        @pl.when(p < z)
        def _():
            for j in range(chunks):
                up(p, j).wait_recv()
                pl.when(z < n - 1)(lambda: up(p, j).start())
                send_across(p, j)

        @pl.when(p == z - 1)
        def _():
            for j in range(chunks):
                late = (z < n - 1) & (j >= 2 * z)
                pl.when(late)(lambda: up(z, j).start())

            @pl.loop(z + 1, jnp.minimum(z + 1 + p, n))
            def _(c):
                for j in range(chunks):
                    send_across(c, j)

        d = z + 1 + p

        @pl.when(d < n)
        def _():
            for j in range(chunks):
                down(d, j).wait_recv()
                pl.when(z > 0)(lambda: down(d, j).start())
                pl.when(p >= z - 1)(lambda: send_across(d, j))

    phase(0)

    @pl.loop(0, n)
    def _(c):
        for j in range(chunks):
            for r in range(1, m):
                across(c, j, r).wait_recv()
        w1, w3, w2 = [state[i].astype(BF16) for i in range(3)]

        @pl.when(c == z)
        def _():
            out_ref[...] = apply_net(q_ref[...], w1, w3, w2)

        k = kv[c, :, :, 0].reshape(m * tok, head)
        nv = kv[c, :, :, 1].reshape(m * tok, head)
        for i, g in enumerate(span_grads(k, nv, w1, w3, w2)):
            grad[i] = g
        phase(c + 1)
        xs = newton([grad[i] for i in range(3)])
        for i in range(3):
            moved = state[i] - step_size * xs[i].astype(BF16).astype(F32)
            after = jnp.sum(moved * moved, axis=0, keepdims=True)
            ratio = (norm[i] + column_eps) / (after + column_eps)
            state[i] = moved * jnp.sqrt(ratio)
            norm[i] = after * ratio

    rows = final_ref.shape[1]
    final_ref[...] = state[:, pl.ds(pl.multiple_of(z * rows, rows), rows), :]

    @pl.loop(0, n)
    def _(c):
        for j in range(chunks):
            pl.when((c <= z) & (z < n - 1))(lambda: up(c, j).wait_send())
            pl.when((c >= z) & (z > 0))(lambda: down(c, j).wait_send())
            for r in range(1, m):
                across(c, j, r).wait_send()


def per_device(queries, keys, values, rates, video_start, span_len, init_weights):
    tok, head = queries.shape[1:]
    n, m = lax.axis_size("seq"), lax.axis_size("inner")
    rows = init_weights.shape[1] // n
    vm = pl.BlockSpec(memory_space=pltpu.VMEM)
    sm = pl.BlockSpec(memory_space=pltpu.SMEM)
    dma = pltpu.SemaphoreType.DMA
    out, final = pl.pallas_call(
        functools.partial(kernel, n, m),
        out_shape=(
            jax.ShapeDtypeStruct((tok, head), BF16),
            jax.ShapeDtypeStruct((3, rows, init_weights.shape[2]), F32),
        ),
        in_specs=[sm, sm, vm, vm, vm, vm, vm],
        out_specs=(vm, vm),
        scratch_shapes=[
            pltpu.VMEM((n, m, CHUNKS, 2, tok // CHUNKS, head), BF16),
            pltpu.VMEM(init_weights.shape, F32),
            pltpu.VMEM((3, 1, init_weights.shape[2]), F32),
            pltpu.VMEM(init_weights.shape, F32),
            dma((n, CHUNKS)),
            dma((n, CHUNKS)),
            dma((n, CHUNKS)),
            dma((m - 1, n, CHUNKS)),
            dma((m - 1, n, CHUNKS)),
        ],
        compiler_params=pltpu.CompilerParams(collective_id=0, has_side_effects=True),
    )(video_start, span_len, keys[0], values[0], rates, queries[0], init_weights)
    return out[None], final[None]


def solution(mesh):
    in_specs = (
        P(("groups", "batch"), ("seq", "inner"), None),
        P(("groups", "batch"), ("seq", "inner"), None),
        P(("groups", "batch"), ("seq", "inner"), None),
        P(("groups", "batch"), ("seq", "inner")),
        P(("groups", "batch")),
        P(("groups", "batch"), "seq"),
        P(),
    )
    out_specs = (
        P(("groups", "batch"), ("seq", "inner"), None),
        P(("groups", "batch"), None, "seq", None),
    )
    return jax.shard_map(
        per_device, mesh=mesh, in_specs=in_specs, out_specs=out_specs, check_vma=False
    )
```

```python
import functools

import jax
import jax.numpy as jnp
from jax import lax
from jax.experimental import pallas as pl
from jax.experimental.pallas import tpu as pltpu
from jax.sharding import PartitionSpec as P

NS_STEPS = 5
CHUNKS = 4
MESH = pl.DeviceIdType.MESH
step_size = 0.1
norm_eps = 1e-07
column_eps = 1e-06
F32, BF16 = jnp.float32, jnp.bfloat16


def dot(a, b, ca, cb):
    return lax.dot_general(a, b, (((ca,), (cb,)), ((), ())), preferred_element_type=F32)


def apply_net(rows, w1, w3, w2):
    gate = dot(rows, w1, 1, 0)
    up = dot(rows, w3, 1, 0)
    hidden = (gate * jax.nn.sigmoid(gate) * up).astype(BF16)
    return dot(hidden, w2, 1, 1).astype(BF16)


def span_grads(k, nv, w1, w3, w2):
    gate = dot(k, w1, 1, 0)
    up = dot(k, w3, 1, 0)
    back = dot(nv, w2, 1, 0)
    s = jax.nn.sigmoid(gate)
    active = gate * s
    hidden = (active * up).astype(BF16)
    d_up = (back * active).astype(BF16)
    d_gate = (back * up * (s * (1.0 + gate * (1.0 - s)))).astype(BF16)
    return [dot(k, d_gate, 0, 0), dot(k, d_up, 0, 0), dot(nv, hidden, 0, 0)]


def newton(grads):
    xs = [g * (1.0 / (jnp.sqrt(jnp.sum(g * g, keepdims=True)) + norm_eps)) for g in grads]
    for unused in range(NS_STEPS):
        halves = [x.astype(BF16) for x in xs]
        grams = [dot(h, h, 1, 1).astype(BF16) for h in halves]
        xs = [1.5 * x - 0.5 * dot(g, h, 1, 0) for x, g, h in zip(xs, grams, halves)]
    return xs


def kernel(
    n, m, start_ref, len_ref, key_ref, value_ref, rate_ref, q_ref, init_ref, out_ref, final_ref,
    kv, queue, outs, state, norm, grad,
    give_send, give_recv, q_send, q_recv, o_send, o_recv, f_send, f_recv, z_recv, up_send, down_send,
):
    z, x = lax.axis_index("seq"), lax.axis_index("inner")
    chief = lax.rem(lax.axis_index("batch"), m)
    place = lax.rem(x - chief + m, m)
    active = place == 0
    tok = key_ref.shape[0]
    chunks, pair, part, head = kv.shape[2:]
    rows = final_ref.shape[1]
    mine = pl.ds(pl.multiple_of(z * rows, rows), rows)

    barrier = pltpu.get_barrier_semaphore()

    def greet(where):
        pl.semaphore_signal(barrier, inc=1, device_id=where, device_id_type=MESH)

    def helper(r):
        return {"inner": lax.rem(chief + r, m)}

    @pl.when(active)
    def _():
        pl.when(z > 0)(lambda: greet({"seq": z - 1}))
        pl.when(z < n - 1)(lambda: greet({"seq": z + 1}))
        for r in range(1, m):
            greet(helper(r))

    @pl.when(jnp.logical_not(active))
    def _():
        greet({"inner": chief})

    within = lax.broadcasted_iota(jnp.int32, (1, tok), 1) + x * tok
    position = within + z * (tok * m)
    valid = ((position >= start_ref[0]) & (within < len_ref[0, 0])).astype(F32)
    weight = rate_ref[...] * valid
    eye = lax.broadcasted_iota(jnp.int32, (tok, tok), 0) == lax.broadcasted_iota(
        jnp.int32, (tok, tok), 1
    )
    column = jnp.sum(jnp.where(eye, weight, 0.0), axis=1, keepdims=True)
    neg = (-(column * value_ref[...].astype(F32))).astype(BF16)
    for j in range(chunks):
        kv[z, place, j, 0] = key_ref[j * part : (j + 1) * part, :]
        kv[z, place, j, 1] = neg[j * part : (j + 1) * part, :]

    def copy(src, dst, send, recv, where):
        return pltpu.make_async_remote_copy(src, dst, send, recv, where, MESH)

    def give(r, j):
        block = kv.at[z, r, j]
        return copy(block, block, give_send.at[j], give_recv.at[r, j], {"inner": chief})

    def give_q(r):
        return copy(q_ref, queue.at[r], q_send.at[0], q_recv.at[r], {"inner": chief})

    def give_out(r):
        return copy(outs.at[r], out_ref, o_send.at[r], o_recv.at[0], helper(r))

    def give_final(r, i):
        return copy(state.at[i, mine], final_ref.at[i], f_send.at[r, i], f_recv.at[i], helper(r))

    def up(c, r, j):
        block = kv.at[c, r, j]
        return copy(block, block, up_send.at[c, r, j], z_recv.at[c, r, j], {"seq": z + 1})

    def down(c, r, j):
        block = kv.at[c, r, j]
        return copy(block, block, down_send.at[c, r, j], z_recv.at[c, r, j], {"seq": z - 1})

    @pl.when(jnp.logical_not(active))
    def _():
        pl.semaphore_wait(barrier, 1)
        for j in range(chunks):
            give(place, j).start()
        give_q(place).start()
        for j in range(chunks):
            give(place, j).wait_send()
        give_q(place).wait_send()
        give_out(0).wait_recv()
        for i in range(3):
            give_final(0, i).wait_recv()

    def relay_up(c, first, last):
        for r in range(first, last):
            for j in range(chunks):
                up(c, r, j).wait_recv()
                pl.when(z < n - 1)(lambda: up(c, r, j).start())

    def phase(p, first):
        pl.when(p < z)(lambda: relay_up(p, first, m))

        @pl.when((p == z - 1) & (z < n - 1))
        def _():
            for r in range(1, m):
                for j in range(chunks):
                    up(z, r, j).start()

        d = z + 1 + p - (z == 0).astype(jnp.int32)

        @pl.when((d < n) & (d > z))
        def _():
            for r in range(m):
                for j in range(chunks):
                    down(d, r, j).wait_recv()
                    pl.when(z > 0)(lambda: down(d, r, j).start())

    @pl.when(active)
    def _():
        for i in range(3):
            w = init_ref[i]
            state[i] = w
            norm[i] = jnp.sum(w * w, axis=0, keepdims=True)
        pl.semaphore_wait(
            barrier, (m - 1) + (z > 0).astype(jnp.int32) + (z < n - 1).astype(jnp.int32)
        )
        for j in range(chunks):
            pl.when(z < n - 1)(lambda: up(z, 0, j).start())
            pl.when(z > 0)(lambda: down(z, 0, j).start())
        pl.when(z > 0)(lambda: relay_up(0, 0, 1))
        for r in range(1, m):
            for j in range(chunks):
                give(r, j).wait_recv()
                pl.when(z == 0)(lambda: up(z, r, j).start())
                pl.when(z > 0)(lambda: down(z, r, j).start())
        phase(0, 1)
        for r in range(1, m):
            give_q(r).wait_recv()

        @pl.loop(0, n)
        def _(c):
            w1, w3, w2 = [state[i].astype(BF16) for i in range(3)]

            @pl.when(c == z)
            def _():
                for r in range(1, m):
                    outs[r] = apply_net(queue[r], w1, w3, w2)
                out_ref[...] = apply_net(q_ref[...], w1, w3, w2)

            k = kv[c, :, :, 0].reshape(m * tok, head)
            nv = kv[c, :, :, 1].reshape(m * tok, head)
            for i, g in enumerate(span_grads(k, nv, w1, w3, w2)):
                grad[i] = g

            @pl.when(c == z)
            def _():
                for r in range(1, m):
                    give_out(r).start()

            phase(c + 1, 0)
            xs = newton([grad[i] for i in range(3)])
            for i in range(3):
                moved = state[i] - step_size * xs[i].astype(BF16).astype(F32)
                after = jnp.sum(moved * moved, axis=0, keepdims=True)
                ratio = (norm[i] + column_eps) / (after + column_eps)
                state[i] = moved * jnp.sqrt(ratio)
                norm[i] = after * ratio

        final_ref[...] = state[:, mine, :]
        for i in range(3):
            for r in range(1, m):
                give_final(r, i).start()

        @pl.loop(0, n)
        def _(c):
            for r in range(m):
                for j in range(chunks):
                    pl.when((c <= z) & (z < n - 1))(lambda: up(c, r, j).wait_send())
                    pl.when((c >= z) & (z > 0))(lambda: down(c, r, j).wait_send())

        for r in range(1, m):
            give_out(r).wait_send()
            for i in range(3):
                give_final(r, i).wait_send()


def per_device(queries, keys, values, rates, video_start, span_len, init_weights):
    tok, head = queries.shape[1:]
    n, m = lax.axis_size("seq"), lax.axis_size("inner")
    hidden = init_weights.shape[2]
    rows = init_weights.shape[1] // n
    vm = pl.BlockSpec(memory_space=pltpu.VMEM)
    sm = pl.BlockSpec(memory_space=pltpu.SMEM)
    dma = pltpu.SemaphoreType.DMA
    out, final = pl.pallas_call(
        functools.partial(kernel, n, m),
        out_shape=(
            jax.ShapeDtypeStruct((tok, head), BF16),
            jax.ShapeDtypeStruct((3, rows, hidden), F32),
        ),
        in_specs=[sm, sm, vm, vm, vm, vm, vm],
        out_specs=(vm, vm),
        scratch_shapes=[
            pltpu.VMEM((n, m, CHUNKS, 2, tok // CHUNKS, head), BF16),
            pltpu.VMEM((m, tok, head), BF16),
            pltpu.VMEM((m, tok, head), BF16),
            pltpu.VMEM(init_weights.shape, F32),
            pltpu.VMEM((3, 1, hidden), F32),
            pltpu.VMEM(init_weights.shape, F32),
            dma((CHUNKS,)),
            dma((m, CHUNKS)),
            dma((1,)),
            dma((m,)),
            dma((m,)),
            dma((1,)),
            dma((m, 3)),
            dma((3,)),
            dma((n, m, CHUNKS)),
            dma((n, m, CHUNKS)),
            dma((n, m, CHUNKS)),
        ],
        compiler_params=pltpu.CompilerParams(collective_id=0, has_side_effects=True),
    )(video_start, span_len, keys[0], values[0], rates, queries[0], init_weights)
    return out[None], final[None]


def solution(mesh):
    in_specs = (
        P(("groups", "batch"), ("seq", "inner"), None),
        P(("groups", "batch"), ("seq", "inner"), None),
        P(("groups", "batch"), ("seq", "inner"), None),
        P(("groups", "batch"), ("seq", "inner")),
        P(("groups", "batch")),
        P(("groups", "batch"), "seq"),
        P(),
    )
    out_specs = (
        P(("groups", "batch"), ("seq", "inner"), None),
        P(("groups", "batch"), None, "seq", None),
    )
    return jax.shard_map(
        per_device, mesh=mesh, in_specs=in_specs, out_specs=out_specs, check_vma=False
    )
```

```python
import functools

import jax
import jax.numpy as jnp
from jax import lax
from jax.experimental import pallas as pl
from jax.experimental.pallas import tpu as pltpu
from jax.sharding import PartitionSpec as P

NS_STEPS = 5
CHUNKS = 4
MESH = pl.DeviceIdType.MESH
step_size = 0.1
norm_eps = 1e-07
column_eps = 1e-06
F32, BF16 = jnp.float32, jnp.bfloat16


def dot(a, b, ca, cb):
    return lax.dot_general(a, b, (((ca,), (cb,)), ((), ())), preferred_element_type=F32)


def apply_net(rows, w1, w3, w2):
    gate = dot(rows, w1, 1, 0)
    up = dot(rows, w3, 1, 0)
    hidden = (gate * jax.nn.sigmoid(gate) * up).astype(BF16)
    return dot(hidden, w2, 1, 1).astype(BF16)


def span_grads(k, nv, w1, w3, w2):
    gate = dot(k, w1, 1, 0)
    up = dot(k, w3, 1, 0)
    back = dot(nv, w2, 1, 0)
    s = jax.nn.sigmoid(gate)
    active = gate * s
    hidden = (active * up).astype(BF16)
    d_up = (back * active).astype(BF16)
    d_gate = (back * up * (s * (1.0 + gate * (1.0 - s)))).astype(BF16)
    return [dot(k, d_gate, 0, 0), dot(k, d_up, 0, 0), dot(nv, hidden, 0, 0)]


def newton(grads):
    xs = [g * (1.0 / (jnp.sqrt(jnp.sum(g * g, keepdims=True)) + norm_eps)) for g in grads]
    for unused in range(NS_STEPS):
        halves = [x.astype(BF16) for x in xs]
        grams = [dot(h, h, 1, 1).astype(BF16) for h in halves]
        xs = [1.5 * x - 0.5 * dot(g, h, 1, 0) for x, g, h in zip(xs, grams, halves)]
    return xs


def kernel(
    n, m, start_ref, len_ref, key_ref, value_ref, rate_ref, q_ref, init_ref, out_ref, final_ref,
    kv, queue, outs, state, norm, grad,
    give_send, give_recv, q_send, q_recv, o_send, o_recv, f_send, f_recv, z_recv, up_send, down_send,
):
    z, x = lax.axis_index("seq"), lax.axis_index("inner")
    chief = lax.rem(lax.axis_index("batch"), m)
    place = lax.rem(x - chief + m, m)
    active = place == 0
    tok = key_ref.shape[0]
    chunks, pair, part, head = kv.shape[2:]
    rows = final_ref.shape[1]
    mine = pl.ds(pl.multiple_of(z * rows, rows), rows)

    barrier = pltpu.get_barrier_semaphore()

    def greet(where):
        pl.semaphore_signal(barrier, inc=1, device_id=where, device_id_type=MESH)

    def helper(r):
        return {"inner": lax.rem(chief + r, m)}

    @pl.when(active)
    def _():
        pl.when(z > 0)(lambda: greet({"seq": z - 1}))
        pl.when(z < n - 1)(lambda: greet({"seq": z + 1}))
        for r in range(1, m):
            greet(helper(r))

    @pl.when(jnp.logical_not(active))
    def _():
        greet({"inner": chief})

    within = lax.broadcasted_iota(jnp.int32, (1, tok), 1) + x * tok
    position = within + z * (tok * m)
    valid = ((position >= start_ref[0]) & (within < len_ref[0, 0])).astype(F32)
    weight = rate_ref[...] * valid
    eye = lax.broadcasted_iota(jnp.int32, (tok, tok), 0) == lax.broadcasted_iota(
        jnp.int32, (tok, tok), 1
    )
    column = jnp.sum(jnp.where(eye, weight, 0.0), axis=1, keepdims=True)
    neg = (-(column * value_ref[...].astype(F32))).astype(BF16)
    for j in range(chunks):
        kv[z, place, j, 0] = key_ref[j * part : (j + 1) * part, :]
        kv[z, place, j, 1] = neg[j * part : (j + 1) * part, :]

    def copy(src, dst, send, recv, where):
        return pltpu.make_async_remote_copy(src, dst, send, recv, where, MESH)

    def give(r, j):
        block = kv.at[z, r, j]
        return copy(block, block, give_send.at[j], give_recv.at[r, j], {"inner": chief})

    def give_q(r):
        return copy(q_ref, queue.at[r], q_send.at[0], q_recv.at[r], {"inner": chief})

    def give_out(r):
        return copy(outs.at[r], out_ref, o_send.at[r], o_recv.at[0], helper(r))

    def give_final(r, i):
        return copy(state.at[i, mine], final_ref.at[i], f_send.at[r, i], f_recv.at[i], helper(r))

    def up(c, r, j):
        block = kv.at[c, r, j]
        return copy(block, block, up_send.at[c, r, j], z_recv.at[c, r, j], {"seq": z + 1})

    def down(c, r, j):
        block = kv.at[c, r, j]
        return copy(block, block, down_send.at[c, r, j], z_recv.at[c, r, j], {"seq": z - 1})

    @pl.when(jnp.logical_not(active))
    def _():
        pl.semaphore_wait(barrier, 1)
        for j in range(chunks):
            give(place, j).start()
        give_q(place).start()
        for j in range(chunks):
            give(place, j).wait_send()
        give_q(place).wait_send()
        give_out(0).wait_recv()
        for i in range(3):
            give_final(0, i).wait_recv()

    def relay_up(c, first, last):
        for r in range(first, last):
            for j in range(chunks):
                up(c, r, j).wait_recv()
                pl.when(z < n - 1)(lambda: up(c, r, j).start())

    def phase(p, first):
        pl.when(p < z)(lambda: relay_up(p, first, m))

        @pl.when((p == z - 1) & (z < n - 1))
        def _():
            for r in range(1, m):
                for j in range(chunks):
                    up(z, r, j).start()

        d = z + p

        @pl.when((d < n) & (d > z))
        def _():
            for r in range(m):
                for j in range(chunks):
                    down(d, r, j).wait_recv()
                    pl.when(z > 0)(lambda: down(d, r, j).start())

    @pl.when(active)
    def _():
        for i in range(3):
            w = init_ref[i]
            state[i] = w
            norm[i] = jnp.sum(w * w, axis=0, keepdims=True)
        pl.semaphore_wait(
            barrier, (m - 1) + (z > 0).astype(jnp.int32) + (z < n - 1).astype(jnp.int32)
        )
        for j in range(chunks):
            pl.when(z < n - 1)(lambda: up(z, 0, j).start())
            pl.when(z > 0)(lambda: down(z, 0, j).start())
        pl.when(z == 1)(lambda: relay_up(0, 0, 1))
        for r in range(1, m):
            for j in range(chunks):
                give(r, j).wait_recv()
                pl.when(z == 0)(lambda: up(z, r, j).start())
                pl.when(z > 0)(lambda: down(z, r, j).start())
        pl.when(z > 1)(lambda: relay_up(0, 0, 1))
        phase(0, 1)
        for r in range(1, m):
            give_q(r).wait_recv()

        @pl.loop(0, n)
        def _(c):
            w1, w3, w2 = [state[i].astype(BF16) for i in range(3)]

            @pl.when(c == z)
            def _():
                for r in range(1, m):
                    outs[r] = apply_net(queue[r], w1, w3, w2)
                out_ref[...] = apply_net(q_ref[...], w1, w3, w2)

            k = kv[c, :, :, 0].reshape(m * tok, head)
            nv = kv[c, :, :, 1].reshape(m * tok, head)
            for i, g in enumerate(span_grads(k, nv, w1, w3, w2)):
                grad[i] = g

            @pl.when(c == z)
            def _():
                for r in range(1, m):
                    give_out(r).start()

            phase(c + 1, 0)
            xs = newton([grad[i] for i in range(3)])
            for i in range(3):
                moved = state[i] - step_size * xs[i].astype(BF16).astype(F32)
                after = jnp.sum(moved * moved, axis=0, keepdims=True)
                ratio = (norm[i] + column_eps) / (after + column_eps)
                state[i] = moved * jnp.sqrt(ratio)
                norm[i] = after * ratio

        final_ref[...] = state[:, mine, :]
        for i in range(3):
            for r in range(1, m):
                give_final(r, i).start()

        @pl.loop(0, n)
        def _(c):
            for r in range(m):
                for j in range(chunks):
                    pl.when((c <= z) & (z < n - 1))(lambda: up(c, r, j).wait_send())
                    pl.when((c >= z) & (z > 0))(lambda: down(c, r, j).wait_send())

        for r in range(1, m):
            give_out(r).wait_send()
            for i in range(3):
                give_final(r, i).wait_send()


def per_device(queries, keys, values, rates, video_start, span_len, init_weights):
    tok, head = queries.shape[1:]
    n, m = lax.axis_size("seq"), lax.axis_size("inner")
    hidden = init_weights.shape[2]
    rows = init_weights.shape[1] // n
    vm = pl.BlockSpec(memory_space=pltpu.VMEM)
    sm = pl.BlockSpec(memory_space=pltpu.SMEM)
    dma = pltpu.SemaphoreType.DMA
    out, final = pl.pallas_call(
        functools.partial(kernel, n, m),
        out_shape=(
            jax.ShapeDtypeStruct((tok, head), BF16),
            jax.ShapeDtypeStruct((3, rows, hidden), F32),
        ),
        in_specs=[sm, sm, vm, vm, vm, vm, vm],
        out_specs=(vm, vm),
        scratch_shapes=[
            pltpu.VMEM((n, m, CHUNKS, 2, tok // CHUNKS, head), BF16),
            pltpu.VMEM((m, tok, head), BF16),
            pltpu.VMEM((m, tok, head), BF16),
            pltpu.VMEM(init_weights.shape, F32),
            pltpu.VMEM((3, 1, hidden), F32),
            pltpu.VMEM(init_weights.shape, F32),
            dma((CHUNKS,)),
            dma((m, CHUNKS)),
            dma((1,)),
            dma((m,)),
            dma((m,)),
            dma((1,)),
            dma((m, 3)),
            dma((3,)),
            dma((n, m, CHUNKS)),
            dma((n, m, CHUNKS)),
            dma((n, m, CHUNKS)),
        ],
        compiler_params=pltpu.CompilerParams(collective_id=0, has_side_effects=True),
    )(video_start, span_len, keys[0], values[0], rates, queries[0], init_weights)
    return out[None], final[None]


def solution(mesh):
    in_specs = (
        P(("groups", "batch"), ("seq", "inner"), None),
        P(("groups", "batch"), ("seq", "inner"), None),
        P(("groups", "batch"), ("seq", "inner"), None),
        P(("groups", "batch"), ("seq", "inner")),
        P(("groups", "batch")),
        P(("groups", "batch"), "seq"),
        P(),
    )
    out_specs = (
        P(("groups", "batch"), ("seq", "inner"), None),
        P(("groups", "batch"), None, "seq", None),
    )
    return jax.shard_map(
        per_device, mesh=mesh, in_specs=in_specs, out_specs=out_specs, check_vma=False
    )
```

```python
import functools

import jax
import jax.numpy as jnp
from jax import lax
from jax.experimental import pallas as pl
from jax.experimental.pallas import tpu as pltpu
from jax.sharding import PartitionSpec as P

NS_STEPS = 5
CHUNKS = 4
MESH = pl.DeviceIdType.MESH
step_size = 0.1
norm_eps = 1e-07
column_eps = 1e-06
F32, BF16 = jnp.float32, jnp.bfloat16


def dot(a, b, ca, cb):
    return lax.dot_general(a, b, (((ca,), (cb,)), ((), ())), preferred_element_type=F32)


def apply_net(rows, w1, w3, w2):
    gate = dot(rows, w1, 1, 0)
    up = dot(rows, w3, 1, 0)
    hidden = (gate * jax.nn.sigmoid(gate) * up).astype(BF16)
    return dot(hidden, w2, 1, 1).astype(BF16)


def span_grads(k, nv, w1, w3, w2):
    gate = dot(k, w1, 1, 0)
    up = dot(k, w3, 1, 0)
    back = dot(nv, w2, 1, 0)
    s = jax.nn.sigmoid(gate)
    active = gate * s
    hidden = (active * up).astype(BF16)
    d_up = (back * active).astype(BF16)
    d_gate = (back * up * (s * (1.0 + gate * (1.0 - s)))).astype(BF16)
    return [dot(k, d_gate, 0, 0), dot(k, d_up, 0, 0), dot(nv, hidden, 0, 0)]


def newton(grads):
    xs = [g * (1.0 / (jnp.sqrt(jnp.sum(g * g, keepdims=True)) + norm_eps)) for g in grads]
    for unused in range(NS_STEPS):
        halves = [x.astype(BF16) for x in xs]
        grams = [dot(h, h, 1, 1).astype(BF16) for h in halves]
        xs = [1.5 * x - 0.5 * dot(g, h, 1, 0) for x, g, h in zip(xs, grams, halves)]
    return xs


def kernel(
    n, m, start_ref, len_ref, key_ref, value_ref, rate_ref, q_ref, init_ref, out_ref, final_ref,
    kv, queue, outs, state, norm, grad,
    give_send, give_recv, q_send, q_recv, o_send, o_recv, f_send, f_recv, z_recv, up_send, down_send,
):
    z, x = lax.axis_index("seq"), lax.axis_index("inner")
    chief = lax.rem(lax.axis_index("batch"), m)
    place = lax.rem(x - chief + m, m)
    active = place == 0
    tok = key_ref.shape[0]
    chunks, pair, part, head = kv.shape[2:]
    rows = final_ref.shape[1]
    mine = pl.ds(pl.multiple_of(z * rows, rows), rows)

    barrier = pltpu.get_barrier_semaphore()

    def greet(where):
        pl.semaphore_signal(barrier, inc=1, device_id=where, device_id_type=MESH)

    def helper(r):
        return {"inner": lax.rem(chief + r, m)}

    @pl.when(active)
    def _():
        pl.when(z > 0)(lambda: greet({"seq": z - 1}))
        pl.when(z < n - 1)(lambda: greet({"seq": z + 1}))
        for r in range(1, m):
            greet(helper(r))

    @pl.when(jnp.logical_not(active))
    def _():
        greet({"inner": chief})

    within = lax.broadcasted_iota(jnp.int32, (1, tok), 1) + x * tok
    position = within + z * (tok * m)
    valid = ((position >= start_ref[0]) & (within < len_ref[0, 0])).astype(F32)
    weight = rate_ref[...] * valid
    eye = lax.broadcasted_iota(jnp.int32, (tok, tok), 0) == lax.broadcasted_iota(
        jnp.int32, (tok, tok), 1
    )
    column = jnp.sum(jnp.where(eye, weight, 0.0), axis=1, keepdims=True)
    neg = (-(column * value_ref[...].astype(F32))).astype(BF16)
    for j in range(chunks):
        kv[z, place, j, 0] = key_ref[j * part : (j + 1) * part, :]
        kv[z, place, j, 1] = neg[j * part : (j + 1) * part, :]

    def copy(src, dst, send, recv, where):
        return pltpu.make_async_remote_copy(src, dst, send, recv, where, MESH)

    def give(r, j):
        block = kv.at[z, r, j]
        return copy(block, block, give_send.at[j], give_recv.at[r, j], {"inner": chief})

    def give_q(r):
        return copy(q_ref, queue.at[r], q_send.at[0], q_recv.at[r], {"inner": chief})

    def give_out(r):
        return copy(outs.at[r], out_ref, o_send.at[r], o_recv.at[0], helper(r))

    def give_final(r, i):
        return copy(state.at[i, mine], final_ref.at[i], f_send.at[r, i], f_recv.at[i], helper(r))

    def up(c, r, j):
        block = kv.at[c, r, j]
        return copy(block, block, up_send.at[c, r, j], z_recv.at[c, r, j], {"seq": z + 1})

    def down(c, r, j):
        block = kv.at[c, r, j]
        return copy(block, block, down_send.at[c, r, j], z_recv.at[c, r, j], {"seq": z - 1})

    @pl.when(jnp.logical_not(active))
    def _():
        pl.semaphore_wait(barrier, 1)
        for j in range(chunks):
            give(place, j).start()
        give_q(place).start()
        for j in range(chunks):
            give(place, j).wait_send()
        give_q(place).wait_send()
        give_out(0).wait_recv()
        for i in range(3):
            give_final(0, i).wait_recv()

    def relay_up(c, first, last):
        for r in range(first, last):
            for j in range(chunks):
                up(c, r, j).wait_recv()
                pl.when(z < n - 1)(lambda: up(c, r, j).start())

    def phase(p, first):
        pl.when(p < z)(lambda: relay_up(p, first, m))

        @pl.when((p == z - 1) & (z < n - 1))
        def _():
            for r in range(1, m):
                for j in range(chunks):
                    up(z, r, j).start()

        d = z + p

        @pl.when((d < n) & (d > z))
        def _():
            for r in range(m):
                for j in range(chunks):
                    down(d, r, j).wait_recv()
                    pl.when(z > 0)(lambda: down(d, r, j).start())

    @pl.when(active)
    def _():
        for i in range(3):
            w = init_ref[i]
            state[i] = w
            norm[i] = jnp.sum(w * w, axis=0, keepdims=True)
        pl.semaphore_wait(
            barrier, (m - 1) + (z > 0).astype(jnp.int32) + (z < n - 1).astype(jnp.int32)
        )
        for j in range(chunks):
            pl.when(z < n - 1)(lambda: up(z, 0, j).start())
            pl.when(z > 0)(lambda: down(z, 0, j).start())
        pl.when(z == 1)(lambda: relay_up(0, 0, 1))
        for r in range(1, m):
            for j in range(chunks):
                give(r, j).wait_recv()
                pl.when(z == 0)(lambda: up(z, r, j).start())
                pl.when(z > 0)(lambda: down(z, r, j).start())
        pl.when(z > 1)(lambda: relay_up(0, 0, 1))
        phase(0, 1)
        for r in range(1, m):
            give_q(r).wait_recv()

        @pl.loop(0, n)
        def _(c):
            w1, w3, w2 = [state[i].astype(BF16) for i in range(3)]

            @pl.when(c == z)
            def _():
                for r in range(1, m):
                    outs[r] = apply_net(queue[r], w1, w3, w2)
                out_ref[...] = apply_net(q_ref[...], w1, w3, w2)

            k = kv[c, :, :, 0].reshape(m * tok, head)
            nv = kv[c, :, :, 1].reshape(m * tok, head)
            for i, g in enumerate(span_grads(k, nv, w1, w3, w2)):
                grad[i] = g

            @pl.when(c == z)
            def _():
                for r in range(1, m):
                    give_out(r).start()

            xs = newton([grad[i] for i in range(3)])
            for i in range(3):
                moved = state[i] - step_size * xs[i].astype(BF16).astype(F32)
                after = jnp.sum(moved * moved, axis=0, keepdims=True)
                ratio = (norm[i] + column_eps) / (after + column_eps)
                state[i] = moved * jnp.sqrt(ratio)
                norm[i] = after * ratio
            phase(c + 1, 0)

        final_ref[...] = state[:, mine, :]
        for i in range(3):
            for r in range(1, m):
                give_final(r, i).start()

        @pl.loop(0, n)
        def _(c):
            for r in range(m):
                for j in range(chunks):
                    pl.when((c <= z) & (z < n - 1))(lambda: up(c, r, j).wait_send())
                    pl.when((c >= z) & (z > 0))(lambda: down(c, r, j).wait_send())

        for r in range(1, m):
            give_out(r).wait_send()
            for i in range(3):
                give_final(r, i).wait_send()


def per_device(queries, keys, values, rates, video_start, span_len, init_weights):
    tok, head = queries.shape[1:]
    n, m = lax.axis_size("seq"), lax.axis_size("inner")
    hidden = init_weights.shape[2]
    rows = init_weights.shape[1] // n
    vm = pl.BlockSpec(memory_space=pltpu.VMEM)
    sm = pl.BlockSpec(memory_space=pltpu.SMEM)
    dma = pltpu.SemaphoreType.DMA
    out, final = pl.pallas_call(
        functools.partial(kernel, n, m),
        out_shape=(
            jax.ShapeDtypeStruct((tok, head), BF16),
            jax.ShapeDtypeStruct((3, rows, hidden), F32),
        ),
        in_specs=[sm, sm, vm, vm, vm, vm, vm],
        out_specs=(vm, vm),
        scratch_shapes=[
            pltpu.VMEM((n, m, CHUNKS, 2, tok // CHUNKS, head), BF16),
            pltpu.VMEM((m, tok, head), BF16),
            pltpu.VMEM((m, tok, head), BF16),
            pltpu.VMEM(init_weights.shape, F32),
            pltpu.VMEM((3, 1, hidden), F32),
            pltpu.VMEM(init_weights.shape, F32),
            dma((CHUNKS,)),
            dma((m, CHUNKS)),
            dma((1,)),
            dma((m,)),
            dma((m,)),
            dma((1,)),
            dma((m, 3)),
            dma((3,)),
            dma((n, m, CHUNKS)),
            dma((n, m, CHUNKS)),
            dma((n, m, CHUNKS)),
        ],
        compiler_params=pltpu.CompilerParams(collective_id=0, has_side_effects=True),
    )(video_start, span_len, keys[0], values[0], rates, queries[0], init_weights)
    return out[None], final[None]


def solution(mesh):
    in_specs = (
        P(("groups", "batch"), ("seq", "inner"), None),
        P(("groups", "batch"), ("seq", "inner"), None),
        P(("groups", "batch"), ("seq", "inner"), None),
        P(("groups", "batch"), ("seq", "inner")),
        P(("groups", "batch")),
        P(("groups", "batch"), "seq"),
        P(),
    )
    out_specs = (
        P(("groups", "batch"), ("seq", "inner"), None),
        P(("groups", "batch"), None, "seq", None),
    )
    return jax.shard_map(
        per_device, mesh=mesh, in_specs=in_specs, out_specs=out_specs, check_vma=False
    )
```
